32 devices in a mesh: grp: 2 (over x), ctx: 16 (over z, y, core).
Axes of the slice: x: 2, y: 2, z: 4, core: 2. Of those that a mesh axis runs over, the one named last changes fastest.
Arguments:
- queries: bfloat16 [2, 24, 64, 576], P('grp', None, 'ctx'), parts along dimension 0, may hold values from -40 to 40
- cache: bfloat16 [2, 8192, 576], P('grp', 'ctx'), parts along dimension 0, may hold values from -6 to 6
- draft_latent: bfloat16 [2, 24, 576], P('grp'), parts along dimension 0, may hold values from -9 to 9
- lengths: int32 [2], P('grp'), parts along dimension 0, may hold values from 4096 to 8192
- parents: int32 [2, 24], P('grp'), parts along dimension 0, may hold values from -1 to 22, as said below
- value_up: bfloat16 [64, 512, 128], P('ctx'), may hold values from -0.25 to 0.25
- out_proj: bfloat16 [8192, 7168], P('ctx'), may hold values from -0.09375 to 0.09375
Outputs:
- attended: bfloat16 [48, 7168], P('grp', 'ctx'), parts along dimension 0
The draws below stay inside these ranges and needn't reach their ends.
There are 2 independent parts, one for each index of `grp`. The reference program is written for one: setup_inputs(seed, part) draws one part's arguments, and reference() takes and returns one part's arrays. A program takes and returns all parts, laid end to end along the dimension named above; an argument that names none is the same for every part. Nothing has to cross between parts.
Inputs may be any that keep to these rules, and one draw needn't show every extreme that they name: parents[r, 0] = -1 and 0 <= parents[r, i] < i for i >= 1.
All inputs are finite; a program needn't handle non-finite values.
Results may differ from the reference program's by a relative error of at most 0.007.
Values may be sent and summed in bfloat16 or wider, within the bound.
A program may use at most 64 MiB of HBM per device.

```python
import math
import jax
import jax.numpy as jnp
from jax import lax

HEADS = 64
LATENT = 512
ROPE_DIM = 64
VALUE_DIM = 128
MODEL = 7168
DRAFT = 24
REQS = 1
CTX_DEV = 512
CTX = 8192
N_CTX = 16


def latent_pack(key):
    base = jax.random.fold_in(key, 71)
    width = LATENT + ROPE_DIM
    noise = jax.random.normal(jax.random.fold_in(base, 1), (REQS, CTX, width), jnp.float32)
    values = jnp.clip(noise, -6.0, 6.0)
    return values


def draw_cache(key, part):
    values = latent_pack(key)
    return values.astype(jnp.bfloat16)


def draw_queries(key, part):
    shape = (REQS, DRAFT, HEADS, LATENT + ROPE_DIM)
    values = jnp.clip(0.83 * jax.random.normal(jax.random.fold_in(key, 81), shape, jnp.float32), -5.0, 5.0)
    return values.astype(jnp.bfloat16)


def draw_parents(key, part):
    picks = jax.random.randint(jax.random.fold_in(key, 91), (REQS, DRAFT), 0, 1 << 20)
    order = jnp.arange(DRAFT, dtype=jnp.int32)[None, :]
    chosen = picks % jnp.maximum(order, 1)
    return jnp.where(order == 0, -1, chosen).astype(jnp.int32)


def strengthened(values, own_key, source, target, blocks, factor):
    def block_of(position):
        return (jnp.arange(values.shape[position]) // (values.shape[position] // blocks)).reshape((-1,) + (1,) * (values.ndim - 1 - position))

    one_side = jax.random.permutation(own_key, blocks)[block_of(target)]
    second = (block_of(target) + blocks // 2) % blocks
    return jnp.where((block_of(source) == one_side) | (block_of(source) == second), factor * values, values)


def steps_of(own_key, dims, cuts, smallest, largest):
    def one(axis_at, blocks):
        steps = jax.random.uniform(jax.random.fold_in(jax.random.fold_in(own_key, 6), axis_at), (blocks,), jnp.float32, smallest / len(cuts), largest / len(cuts))
        return jnp.repeat(jnp.exp(steps), dims[axis_at] // blocks).reshape((-1,) + (1,) * (len(dims) - axis_at - 1))

    level = one(*cuts[0])
    for cut in cuts[1:]:
        level = level * one(*cut)
    return level


def normal_values(key, shape, scale, most, split=(), kind=jnp.bfloat16):
    factor_of = steps_of(key, shape, split, -0.22, 0.18) if split else 1.0
    values = jax.random.normal(key, shape, jnp.float32) * scale * factor_of
    return jnp.minimum(jnp.maximum(values, -most), most).astype(kind)


def heavy_noise(key, shape, spread, most, split, heavy, kind=jnp.bfloat16):
    entries = spread * jax.random.normal(key, shape, jnp.float32)
    if split:
        entries = entries * steps_of(key, shape, split, -0.22, 0.18)
    return jnp.clip(strengthened(entries, jax.random.fold_in(key, 3), *heavy), -most, most).astype(kind)


def setup_inputs(seed: int = 0, part: int = 0) -> dict:
    key_of = jax.random.split(jax.random.key(seed), 8)
    own_keys = jax.random.split(jax.random.fold_in(key_of[7], part), 8)
    return {
        "queries": draw_queries(jax.random.fold_in(jax.random.fold_in(key_of[7], part), 71), part),
        "cache": draw_cache(jax.random.fold_in(jax.random.fold_in(key_of[7], part), 71), part),
        "draft_latent": normal_values(own_keys[2], (REQS, DRAFT, LATENT + ROPE_DIM), 1.5, 9.0),
        "lengths": jax.random.randint(own_keys[3], (REQS,), CTX // 2, CTX + 1).astype(jnp.int32),
        "parents": draw_parents(jax.random.fold_in(jax.random.fold_in(key_of[7], part), 71), part),
        "value_up": normal_values(key_of[5], (HEADS, LATENT, VALUE_DIM), LATENT ** -0.5, 0.25, ((0, 16),)),
        "out_proj": heavy_noise(key_of[6], (HEADS * VALUE_DIM, MODEL), (HEADS * VALUE_DIM) ** -0.5, 0.09375, ((0, 16),), (0, 1, 16, 2.0)),
    }


yarn_factor = 1.0 + 0.1 * math.log(32.0)
score_scale = yarn_factor * yarn_factor / math.sqrt(192.0)
neg_fill = -1e+30

def tree_reach(parents):
    drafts = parents.shape[1]
    order = jnp.arange(drafts, dtype=jnp.int32)
    adjacent = (parents[:, :, None] == order[None, None, :]).astype(jnp.float32)
    ident = jnp.broadcast_to(jnp.eye(drafts, dtype=jnp.float32), adjacent.shape)

    def extend(step, reach):
        grown = ident + jnp.einsum('rij,rjk->rik', adjacent, reach, precision=lax.Precision.HIGHEST)
        return jnp.minimum(grown, 1.0)
    return lax.fori_loop(0, drafts, extend, ident) > 0.5

def single_state(rows, keys, valid):
    scores = lax.dot_general(rows, keys, (((1,), (1,)), ((), ())), preferred_element_type=jnp.float32) * score_scale
    masked = jnp.where(valid, scores, neg_fill)
    top = lax.optimization_barrier(jnp.max(masked, axis=1))
    weights = jnp.where(valid, jnp.exp(masked - top[:, None]), 0.0).astype(jnp.bfloat16)
    numer = jnp.dot(weights, keys[:, :LATENT], preferred_element_type=jnp.float32)
    total = lax.optimization_barrier(jnp.sum(weights.astype(jnp.float32), axis=1))
    return (numer, top, total)

def join(first, second):
    best = jnp.maximum(first[1], second[1])
    factor_a = jnp.exp(first[1] - best)
    factor_b = jnp.exp(second[1] - best)
    return (first[0] * factor_a[..., None] + second[0] * factor_b[..., None], best, first[2] * factor_a + second[2] * factor_b)

def reference(queries, cache, draft_latent, lengths, parents, value_up, out_proj):
    reach = tree_reach(parents)
    pieces = []
    for request in range(REQS):
        rows = queries[request].reshape(DRAFT * HEADS, LATENT + ROPE_DIM)
        blocks = cache[request].reshape(N_CTX, CTX_DEV, LATENT + ROPE_DIM)
        starts = jnp.arange(N_CTX, dtype=jnp.int32) * CTX_DEV
        limit = lengths[request]
        start_state = (jnp.zeros((DRAFT * HEADS, LATENT), jnp.float32), jnp.full((DRAFT * HEADS,), neg_fill, jnp.float32), jnp.zeros((DRAFT * HEADS,), jnp.float32))

        def fold(state, item):
            keys, first = item
            live = (first + jnp.arange(CTX_DEV, dtype=jnp.int32) < limit)[None, :]
            return (join(state, single_state(rows, keys, live)), None)
        state, unused = lax.scan(fold, start_state, (blocks, starts))
        tree = jnp.repeat(reach[request], HEADS, axis=0)
        state = join(state, single_state(rows, draft_latent[request], tree))
        latent_out = (state[0] / state[2][:, None]).astype(jnp.bfloat16).reshape(DRAFT, HEADS, LATENT)
        values = jnp.einsum('dhl,hlv->dhv', latent_out.astype(jnp.float32), value_up.astype(jnp.float32), precision=lax.Precision.HIGHEST).astype(jnp.bfloat16)
        pieces.append(values.reshape(DRAFT, HEADS * VALUE_DIM))
    flat = jnp.concatenate(pieces, axis=0)
    return jnp.dot(flat, out_proj, preferred_element_type=jnp.float32).astype(jnp.bfloat16)
```

```python
import functools
import math

import jax
import jax.numpy as jnp
from jax import lax
from jax.experimental import pallas as pl
from jax.experimental.pallas import tpu as pltpu
from jax.sharding import PartitionSpec as P

yarn_factor = 1.0 + 0.1 * math.log(32.0)
score_scale = yarn_factor * yarn_factor / math.sqrt(192.0)
neg_fill = -1e30
MESH = pl.DeviceIdType.MESH
pieces = 4


def dot_nt(a, b):
    return lax.dot_general(a, b, (((1,), (1,)), ((), ())), preferred_element_type=jnp.float32)


def dot_nn(a, b):
    return lax.dot_general(a, b, (((1,), (0,)), ((), ())), preferred_element_type=jnp.float32)


def kernel(
    n, quad, heads, drafts, latent, width, vdim,
    q_hbm, cache_hbm, draft_hbm, lengths_ref, parents_ref, up_hbm, proj_hbm,
    out_ref,
    qbuf, kv, draft, up, proj, acc, state_out, state_in, stat_out, stat_in, share_out, share_in,
    load_sem, own_send, own_recv, near_send, near_recv, relay_send, relay_recv,
    q_send, q_recv, st_send, st_recv, stat_send, stat_recv, share_send, share_recv,
):
    me = lax.axis_index("ctx")
    depth = n // quad
    rows = drafts * heads
    block = cache_hbm.shape[0]
    piece = block // pieces
    z = lax.div(me, quad)
    q = lax.rem(me, quad)
    core = lax.rem(q, 2)
    other = q + 1 - 2 * core
    partner = z * quad + other
    two_chips = quad > 2
    near_q = lax.rem(q + 2, quad)
    near = z * quad + near_q
    near_other_q = near_q + 1 - 2 * core

    def load(src, dst, i):
        copy = pltpu.make_async_copy(src, dst, load_sem.at[i])
        copy.start()
        return copy

    get_kv = load(cache_hbm, kv.at[0], 0)
    get_q = load(q_hbm, qbuf.at[0], 1)
    get_draft = load(draft_hbm, draft, 2)
    get_up = load(up_hbm, up, 3)
    get_proj = load(proj_hbm, proj, 4)

    barrier = pltpu.get_barrier_semaphore()
    for o in range(1, n):
        pl.semaphore_signal(
            barrier, inc=1, device_id={"ctx": lax.rem(me + o, n)}, device_id_type=MESH
        )
    pl.semaphore_wait(barrier, n - 1)

    def remote(src, dst, send, recv, device):
        copy = pltpu.make_async_remote_copy(
            src_ref=src, dst_ref=dst, send_sem=send, recv_sem=recv,
            device_id={"ctx": device}, device_id_type=MESH,
        )
        copy.start()
        return copy

    sent = []
    near_copies = []
    if two_chips:
        for c in range(pieces):
            part = pl.ds(c * piece, piece)
            near_copies.append(remote(
                cache_hbm.at[part], kv.at[2, part], near_send.at[c], near_recv.at[c], near
            ))
    q_copies = []
    for o in range(1, depth):
        dest = lax.rem(z + o, depth) * quad + q
        q_copies.append(remote(q_hbm, qbuf.at[o], q_send.at[o], q_recv.at[o], dest))
    own = remote(cache_hbm, kv.at[1], own_send, own_recv, partner)

    row_id = lax.broadcasted_iota(jnp.int32, (drafts, drafts), 0)
    col_id = lax.broadcasted_iota(jnp.int32, (drafts, drafts), 1)
    eye = jnp.where(row_id == col_id, 1.0, 0.0)
    reach = jnp.where(row_id == jnp.broadcast_to(parents_ref[...], (drafts, drafts)), 1.0, eye)
    for _ in range(max(1, math.ceil(math.log2(drafts)))):
        low = reach.astype(jnp.bfloat16)
        reach = jnp.minimum(dot_nn(low, low), 1.0)
    reach = lax.dot_general(
        reach.astype(jnp.bfloat16), eye.astype(jnp.bfloat16), (((0,), (0,)), ((), ())),
        preferred_element_type=jnp.float32,
    )
    tree = jnp.concatenate([reach] * heads, axis=0) > 0.5
    get_q.wait()
    get_draft.wait()
    keys = draft[...]
    d_score = jnp.where(tree, dot_nt(qbuf[0], keys) * score_scale, neg_fill)
    d_top = jnp.max(d_score, axis=1, keepdims=True)
    d_weight = jnp.where(tree, jnp.exp(d_score - d_top), 0.0).astype(jnp.bfloat16)
    d_total = jnp.sum(d_weight.astype(jnp.float32), axis=1, keepdims=True)
    d_numer = dot_nn(d_weight, keys[:, :latent])

    relays = []

    def relay(c):
        if two_chips:
            part = pl.ds(c * piece, piece)
            near_copies[c].wait_recv()
            relays.append(remote(
                kv.at[2, part], kv.at[3, part], relay_send.at[c], relay_recv.at[c], partner
            ))

    limit = lengths_ref[0]
    joined = rows % 8 == 0 and depth <= 8
    groups = [(0, depth)] if joined else [(o, 1) for o in range(depth)]
    tops = {}
    totals = {}

    def attend(slot, owner_q):
        first = (z * quad + owner_q) * block
        live = (first + lax.broadcasted_iota(jnp.int32, (1, block), 1)) < limit
        for base, count in groups:
            span = count * rows
            query = qbuf[pl.ds(base, count)].reshape(span, width)
            scores = jnp.where(live, dot_nt(query, kv[slot]) * score_scale, neg_fill)
            top = jnp.max(scores, axis=1, keepdims=True)
            place = pl.ds(base * rows, span)
            if base in tops:
                best = jnp.maximum(tops[base], top)
                decay = jnp.exp(tops[base] - best)
            else:
                best = top
            weights = jnp.where(live, jnp.exp(scores - best), 0.0).astype(jnp.bfloat16)
            total = jnp.sum(weights.astype(jnp.float32), axis=1, keepdims=True)
            numer = dot_nn(weights, kv[slot, :, pl.ds(0, latent)])
            if base in tops:
                totals[base] = totals[base] * decay + total
                acc[place] = acc[place] * decay + numer
            else:
                totals[base] = total
                acc[place] = numer
            tops[base] = best

    for c in range(0, pieces - 2):
        relay(c)
    for copy in q_copies:
        copy.wait_recv()
    get_kv.wait()
    attend(0, q)
    own.wait_recv()
    relay(pieces - 2)
    attend(1, other)
    relay(pieces - 1)
    if two_chips:
        attend(2, near_q)
        for copy in relays:
            copy.wait_recv()
        attend(3, near_other_q)

    lane = lax.broadcasted_iota(jnp.int32, (rows, 128), 1)
    fill = jnp.zeros((128 - rows, 128), jnp.float32)
    state_copies = []
    stat_copies = []

    def stats_of(o):
        base, count = next(g for g in groups if g[0] <= o < g[0] + g[1])
        at = (o - base) * rows
        return tops[base][at : at + rows], totals[base][at : at + rows]

    for o in range(1, depth):
        top, total = stats_of(o)
        state_out[o] = acc[pl.ds(o * rows, rows)].astype(jnp.bfloat16)
        column = jnp.where(lane == 0, top, jnp.where(lane == 1, total, 0.0))
        stat_out[o] = jnp.concatenate([column, fill], axis=0).T[:8]
        back = depth - o
        dest = lax.rem(z + back, depth) * quad + q
        state_copies.append(remote(
            state_out.at[o], state_in.at[back], st_send.at[o], st_recv.at[back], dest
        ))
        stat_copies.append(remote(
            stat_out.at[o], stat_in.at[back], stat_send.at[o], stat_recv.at[back], dest
        ))

    def arrived(buf, send, recv, slot):
        return pltpu.make_async_remote_copy(
            src_ref=buf.at[slot], dst_ref=buf.at[slot], send_sem=send.at[slot],
            recv_sem=recv.at[slot], device_id={"ctx": partner}, device_id_type=MESH,
        )

    top0, total0 = stats_of(0)
    for s in range(1, depth):
        arrived(stat_in, stat_send, stat_recv, s).wait_recv()
    shown = jnp.concatenate(
        [stat_in[s] for s in range(1, depth)]
        + [jnp.zeros((-(depth - 1) * 8 % 128, 128), jnp.float32)], axis=0
    ).T
    their_top = [None] + [shown[:rows, 8 * s : 8 * s + 1] for s in range(depth - 1)]
    their_total = [None] + [shown[:rows, 8 * s + 1 : 8 * s + 2] for s in range(depth - 1)]
    best = jnp.maximum(top0, d_top)
    for s in range(1, depth):
        best = jnp.maximum(best, their_top[s])
    f0, fd = jnp.exp(top0 - best), jnp.exp(d_top - best)
    total = total0 * f0 + d_total * fd
    numer = acc[pl.ds(0, rows)] * f0 + d_numer * fd
    for s in range(1, depth):
        factor = jnp.exp(their_top[s] - best)
        total = total + their_total[s] * factor
        arrived(state_in, st_send, st_recv, s).wait_recv()
        numer = numer + state_in[s].astype(jnp.float32) * factor
    latent_out = (numer / total).astype(jnp.bfloat16).astype(jnp.float32)

    get_up.wait()
    values = [
        dot_nn(
            latent_out[h * drafts : (h + 1) * drafts].astype(jnp.bfloat16), up[h]
        ).astype(jnp.bfloat16)
        for h in range(heads)
    ]
    flat = jnp.concatenate(values, axis=1) if heads > 1 else values[0]

    cols = share_in.shape[2]
    per = 128 // math.gcd(cols, 128)
    n_groups = n // per
    mine, seat = lax.div(me, per), lax.rem(me, per)
    get_proj.wait()
    share_copies = []
    for j in list(range(1, n_groups)) + [0]:
        target = lax.rem(mine + j, n_groups)
        start = pl.multiple_of(target * (per * cols), 128)
        product = dot_nn(flat, proj[:, pl.ds(start, per * cols)])
        for t in range(per):
            shifted = product if t == 0 else pltpu.roll(product, per * cols - t * cols, 1)
            share_out[j * per + t] = shifted[:, :cols].astype(jnp.bfloat16)
        if j > 0:
            for t in range(per):
                slot = j * per + seat
                share_copies.append(remote(
                    share_out.at[j * per + t], share_in.at[slot],
                    share_send.at[j * per + t], share_recv.at[slot], target * per + t,
                ))
        else:
            for s in range(1, per):
                t = lax.rem(seat + s, per)
                share_copies.append(remote(
                    share_out.at[t], share_in.at[s],
                    share_send.at[s], share_recv.at[s], mine * per + t,
                ))
    result = share_out[seat].astype(jnp.float32)
    for s in list(range(1, per)) + list(range(per, n)):
        arrived(share_in, share_send, share_recv, s).wait_recv()
        result = result + share_in[s].astype(jnp.float32)
    out_ref[...] = result.astype(jnp.bfloat16)

    own.wait_send()
    for copy in near_copies + relays + q_copies + state_copies + stat_copies + share_copies:
        copy.wait_send()


def on_device(quad, n, queries, cache, draft_latent, lengths, parents, value_up, out_proj):
    _, drafts, heads, width = queries.shape
    block = cache.shape[1]
    latent, vdim = value_up.shape[1:]
    depth = n // quad
    rows = drafts * heads
    model = out_proj.shape[1]
    cols = model // n
    ordered = jnp.swapaxes(queries[0], 0, 1).reshape(rows, width)
    anywhere = pl.BlockSpec(memory_space=pl.ANY)
    in_vmem = pl.BlockSpec(memory_space=pltpu.VMEM)
    in_smem = pl.BlockSpec(memory_space=pltpu.SMEM)
    dma = pltpu.SemaphoreType.DMA
    bf16 = jnp.bfloat16
    return pl.pallas_call(
        functools.partial(kernel, n, quad, heads, drafts, latent, width, vdim),
        out_shape=jax.ShapeDtypeStruct((drafts, cols), bf16),
        in_specs=[anywhere, anywhere, anywhere, in_smem, in_vmem, anywhere, anywhere],
        out_specs=in_vmem,
        scratch_shapes=[
            pltpu.VMEM((depth, rows, width), bf16),
            pltpu.VMEM((quad, block, width), bf16),
            pltpu.VMEM((drafts, width), bf16),
            pltpu.VMEM((heads, latent, vdim), bf16),
            pltpu.VMEM((heads * vdim, model), bf16),
            pltpu.VMEM((depth * rows, latent), jnp.float32),
            pltpu.VMEM((depth, rows, latent), bf16),
            pltpu.VMEM((depth, rows, latent), bf16),
            pltpu.VMEM((depth, 8, 128), jnp.float32),
            pltpu.VMEM((depth, 8, 128), jnp.float32),
            pltpu.VMEM((n, drafts, cols), bf16),
            pltpu.VMEM((n, drafts, cols), bf16),
            dma((5,)),
            dma, dma,
            dma((pieces,)), dma((pieces,)),
            dma((pieces,)), dma((pieces,)),
            dma((depth,)), dma((depth,)),
            dma((depth,)), dma((depth,)),
            dma((depth,)), dma((depth,)),
            dma((n,)), dma((n,)),
        ],
        compiler_params=pltpu.CompilerParams(
            collective_id=0, has_side_effects=True, vmem_limit_bytes=56 * 1024 * 1024
        ),
    )(ordered, cache[0], draft_latent[0], lengths, parents, value_up, out_proj)


def quad_of(mesh):
    line = mesh.devices.reshape(mesh.shape["grp"], mesh.shape["ctx"])[0]
    depth = len({d.coords[2] for d in line})
    return len(line) // depth


def solution(mesh):
    in_specs = (
        P("grp", None, "ctx", None),
        P("grp", "ctx", None),
        P("grp", None, None),
        P("grp"),
        P("grp", None),
        P("ctx", None, None),
        P("ctx", None),
    )
    out_specs = P("grp", "ctx")
    return jax.shard_map(
        functools.partial(on_device, quad_of(mesh), mesh.shape["ctx"]),
        mesh=mesh, in_specs=in_specs, out_specs=out_specs, check_vma=False,
    )
```

```python
import functools
import math

import jax
import jax.numpy as jnp
from jax import lax
from jax.experimental import pallas as pl
from jax.experimental.pallas import tpu as pltpu
from jax.sharding import PartitionSpec as P

yarn_factor = 1.0 + 0.1 * math.log(32.0)
score_scale = yarn_factor * yarn_factor / math.sqrt(192.0)
neg_fill = -1e30
MESH = pl.DeviceIdType.MESH
pieces = 4


def dot_nt(a, b):
    return lax.dot_general(a, b, (((1,), (1,)), ((), ())), preferred_element_type=jnp.float32)


def dot_nn(a, b):
    return lax.dot_general(a, b, (((1,), (0,)), ((), ())), preferred_element_type=jnp.float32)


def kernel(
    n, quad, heads, drafts, latent, width, vdim,
    q_hbm, cache_hbm, draft_hbm, lengths_ref, parents_ref, up_hbm, proj_hbm,
    out_ref,
    qraw, qsplit, qbuf, kv, draft, up, proj, acc, state_out, state_in, stat_out, stat_in, share_out, share_in,
    load_sem, own_send, own_recv, near_send, near_recv, relay_send, relay_recv,
    q_send, q_recv, st_send, st_recv, stat_send, stat_recv, share_send, share_recv,
):
    me = lax.axis_index("ctx")
    depth = n // quad
    rows = drafts * heads
    block = cache_hbm.shape[1]
    piece = width // pieces
    z = lax.div(me, quad)
    q = lax.rem(me, quad)
    core = lax.rem(q, 2)
    other = q + 1 - 2 * core
    partner = z * quad + other
    two_chips = quad > 2
    near_q = lax.rem(q + 2, quad)
    near = z * quad + near_q
    near_other_q = near_q + 1 - 2 * core

    def load(src, dst, i):
        copy = pltpu.make_async_copy(src, dst, load_sem.at[i])
        copy.start()
        return copy

    get_kv = load(cache_hbm, kv.at[0], 0)
    get_q = load(q_hbm, qraw, 1)
    get_draft = load(draft_hbm, draft, 2)
    get_up = load(up_hbm, up, 3)
    get_proj = load(proj_hbm, proj, 4)

    barrier = pltpu.get_barrier_semaphore()
    for o in range(1, n):
        pl.semaphore_signal(
            barrier, inc=1, device_id={"ctx": lax.rem(me + o, n)}, device_id_type=MESH
        )

    get_q.wait()
    for i in range(drafts):
        line = qraw[i].astype(jnp.float32)
        for c in range(0, width, 128):
            lanes = min(128, width - c)
            qsplit[c // 128, pl.ds(i * heads, heads), pl.ds(0, lanes)] = line[:, c : c + lanes]
    for h in range(heads):
        for c in range(0, width, 128):
            lanes = min(128, width - c)
            turned = qsplit[c // 128, pl.ds(h, drafts, stride=heads), :]
            qbuf[0, pl.ds(h * drafts, drafts), pl.ds(c, lanes)] = turned[:, :lanes].astype(
                jnp.bfloat16
            )

    pl.semaphore_wait(barrier, n - 1)

    def remote(src, dst, send, recv, device):
        copy = pltpu.make_async_remote_copy(
            src_ref=src, dst_ref=dst, send_sem=send, recv_sem=recv,
            device_id={"ctx": device}, device_id_type=MESH,
        )
        copy.start()
        return copy

    sent = []
    near_copies = []
    if two_chips:
        for c in range(pieces):
            part = pl.ds(c * piece, piece)
            near_copies.append(remote(
                cache_hbm.at[part], kv.at[2, part], near_send.at[c], near_recv.at[c], near
            ))
    q_copies = []
    for o in range(1, depth):
        dest = lax.rem(z + o, depth) * quad + q
        q_copies.append(remote(qbuf.at[0], qbuf.at[o], q_send.at[o], q_recv.at[o], dest))
    own = remote(cache_hbm, kv.at[1], own_send, own_recv, partner)

    row_id = lax.broadcasted_iota(jnp.int32, (drafts, drafts), 0)
    col_id = lax.broadcasted_iota(jnp.int32, (drafts, drafts), 1)
    eye = jnp.where(row_id == col_id, 1.0, 0.0)
    reach = jnp.where(row_id == jnp.broadcast_to(parents_ref[...], (drafts, drafts)), 1.0, eye)
    for _ in range(max(1, math.ceil(math.log2(drafts)))):
        low = reach.astype(jnp.bfloat16)
        reach = jnp.minimum(dot_nn(low, low), 1.0)
    reach = lax.dot_general(
        reach.astype(jnp.bfloat16), eye.astype(jnp.bfloat16), (((0,), (0,)), ((), ())),
        preferred_element_type=jnp.float32,
    )
    tree = jnp.concatenate([reach] * heads, axis=0) > 0.5
    get_draft.wait()
    keys = draft[...]
    d_score = jnp.where(tree, dot_nt(qbuf[0], keys) * score_scale, neg_fill)
    d_top = jnp.max(d_score, axis=1, keepdims=True)
    d_weight = jnp.where(tree, jnp.exp(d_score - d_top), 0.0).astype(jnp.bfloat16)
    d_total = jnp.sum(d_weight.astype(jnp.float32), axis=1, keepdims=True)
    d_numer = dot_nn(d_weight, keys[:, :latent])

    relays = []

    def relay(c):
        if two_chips:
            part = pl.ds(c * piece, piece)
            near_copies[c].wait_recv()
            relays.append(remote(
                kv.at[2, part], kv.at[3, part], relay_send.at[c], relay_recv.at[c], partner
            ))

    limit = lengths_ref[0]
    joined = rows % 8 == 0 and depth <= 8
    groups = [(0, depth)] if joined else [(o, 1) for o in range(depth)]
    tops = {}
    totals = {}

    def attend(slot, owner_q):
        first = (z * quad + owner_q) * block
        live = (first + lax.broadcasted_iota(jnp.int32, (1, block), 1)) < limit
        for base, count in groups:
            span = count * rows
            query = qbuf[pl.ds(base, count)].reshape(span, width)
            scores = jnp.where(live, dot_nn(query, kv[slot]) * score_scale, neg_fill)
            top = jnp.max(scores, axis=1, keepdims=True)
            place = pl.ds(base * rows, span)
            if base in tops:
                best = jnp.maximum(tops[base], top)
                decay = jnp.exp(tops[base] - best)
            else:
                best = top
            weights = jnp.where(live, jnp.exp(scores - best), 0.0).astype(jnp.bfloat16)
            total = jnp.sum(weights.astype(jnp.float32), axis=1, keepdims=True)
            numer = dot_nt(weights, kv[slot, pl.ds(0, latent), :])
            if base in tops:
                totals[base] = totals[base] * decay + total
                acc[place] = acc[place] * decay + numer
            else:
                totals[base] = total
                acc[place] = numer
            tops[base] = best

    for c in range(0, pieces - 2):
        relay(c)
    for copy in q_copies:
        copy.wait_recv()
    get_kv.wait()
    attend(0, q)
    own.wait_recv()
    relay(pieces - 2)
    attend(1, other)
    relay(pieces - 1)
    if two_chips:
        attend(2, near_q)
        for copy in relays:
            copy.wait_recv()
        attend(3, near_other_q)

    lane = lax.broadcasted_iota(jnp.int32, (rows, 128), 1)
    fill = jnp.zeros((128 - rows, 128), jnp.float32)
    state_copies = []
    stat_copies = []

    def stats_of(o):
        base, count = next(g for g in groups if g[0] <= o < g[0] + g[1])
        at = (o - base) * rows
        return tops[base][at : at + rows], totals[base][at : at + rows]

    for o in range(1, depth):
        top, total = stats_of(o)
        state_out[o] = acc[pl.ds(o * rows, rows)].astype(jnp.bfloat16)
        column = jnp.where(lane == 0, top, jnp.where(lane == 1, total, 0.0))
        stat_out[o] = jnp.concatenate([column, fill], axis=0).T[:8]
        back = depth - o
        dest = lax.rem(z + back, depth) * quad + q
        state_copies.append(remote(
            state_out.at[o], state_in.at[back], st_send.at[o], st_recv.at[back], dest
        ))
        stat_copies.append(remote(
            stat_out.at[o], stat_in.at[back], stat_send.at[o], stat_recv.at[back], dest
        ))

    def arrived(buf, send, recv, slot):
        return pltpu.make_async_remote_copy(
            src_ref=buf.at[slot], dst_ref=buf.at[slot], send_sem=send.at[slot],
            recv_sem=recv.at[slot], device_id={"ctx": partner}, device_id_type=MESH,
        )

    top0, total0 = stats_of(0)
    for s in range(1, depth):
        arrived(stat_in, stat_send, stat_recv, s).wait_recv()
    shown = jnp.concatenate(
        [stat_in[s] for s in range(1, depth)]
        + [jnp.zeros((-(depth - 1) * 8 % 128, 128), jnp.float32)], axis=0
    ).T
    their_top = [None] + [shown[:rows, 8 * s : 8 * s + 1] for s in range(depth - 1)]
    their_total = [None] + [shown[:rows, 8 * s + 1 : 8 * s + 2] for s in range(depth - 1)]
    best = jnp.maximum(top0, d_top)
    for s in range(1, depth):
        best = jnp.maximum(best, their_top[s])
    f0, fd = jnp.exp(top0 - best), jnp.exp(d_top - best)
    total = total0 * f0 + d_total * fd
    numer = acc[pl.ds(0, rows)] * f0 + d_numer * fd
    for s in range(1, depth):
        factor = jnp.exp(their_top[s] - best)
        total = total + their_total[s] * factor
        arrived(state_in, st_send, st_recv, s).wait_recv()
        numer = numer + state_in[s].astype(jnp.float32) * factor
    latent_out = (numer / total).astype(jnp.bfloat16).astype(jnp.float32)

    get_up.wait()
    values = [
        dot_nn(
            latent_out[h * drafts : (h + 1) * drafts].astype(jnp.bfloat16), up[h]
        ).astype(jnp.bfloat16)
        for h in range(heads)
    ]
    flat = jnp.concatenate(values, axis=1) if heads > 1 else values[0]

    cols = share_in.shape[2]
    per = 128 // math.gcd(cols, 128)
    n_groups = n // per
    mine, seat = lax.div(me, per), lax.rem(me, per)
    get_proj.wait()
    share_copies = []
    for j in list(range(1, n_groups)) + [0]:
        target = lax.rem(mine + j, n_groups)
        start = pl.multiple_of(target * (per * cols), 128)
        product = dot_nn(flat, proj[:, pl.ds(start, per * cols)])
        for t in range(per):
            shifted = product if t == 0 else pltpu.roll(product, per * cols - t * cols, 1)
            share_out[j * per + t] = shifted[:, :cols].astype(jnp.bfloat16)
        if j > 0:
            for t in range(per):
                slot = j * per + seat
                share_copies.append(remote(
                    share_out.at[j * per + t], share_in.at[slot],
                    share_send.at[j * per + t], share_recv.at[slot], target * per + t,
                ))
        else:
            for s in range(1, per):
                t = lax.rem(seat + s, per)
                share_copies.append(remote(
                    share_out.at[t], share_in.at[s],
                    share_send.at[s], share_recv.at[s], mine * per + t,
                ))
    result = share_out[seat].astype(jnp.float32)
    for s in list(range(1, per)) + list(range(per, n)):
        arrived(share_in, share_send, share_recv, s).wait_recv()
        result = result + share_in[s].astype(jnp.float32)
    out_ref[...] = result.astype(jnp.bfloat16)

    own.wait_send()
    for copy in near_copies + relays + q_copies + state_copies + stat_copies + share_copies:
        copy.wait_send()


def on_device(quad, n, queries, cache, draft_latent, lengths, parents, value_up, out_proj):
    _, drafts, heads, width = queries.shape
    block = cache.shape[1]
    latent, vdim = value_up.shape[1:]
    depth = n // quad
    rows = drafts * heads
    model = out_proj.shape[1]
    cols = model // n
    anywhere = pl.BlockSpec(memory_space=pl.ANY)
    in_vmem = pl.BlockSpec(memory_space=pltpu.VMEM)
    in_smem = pl.BlockSpec(memory_space=pltpu.SMEM)
    dma = pltpu.SemaphoreType.DMA
    bf16 = jnp.bfloat16
    return pl.pallas_call(
        functools.partial(kernel, n, quad, heads, drafts, latent, width, vdim),
        out_shape=jax.ShapeDtypeStruct((drafts, cols), bf16),
        in_specs=[anywhere, anywhere, anywhere, in_smem, in_vmem, anywhere, anywhere],
        out_specs=in_vmem,
        scratch_shapes=[
            pltpu.VMEM((drafts, heads, width), bf16),
            pltpu.VMEM((pl.cdiv(width, 128), rows, 128), jnp.float32),
            pltpu.VMEM((depth, rows, width), bf16),
            pltpu.VMEM((quad, width, block), bf16),
            pltpu.VMEM((drafts, width), bf16),
            pltpu.VMEM((heads, latent, vdim), bf16),
            pltpu.VMEM((heads * vdim, model), bf16),
            pltpu.VMEM((depth * rows, latent), jnp.float32),
            pltpu.VMEM((depth, rows, latent), bf16),
            pltpu.VMEM((depth, rows, latent), bf16),
            pltpu.VMEM((depth, 8, 128), jnp.float32),
            pltpu.VMEM((depth, 8, 128), jnp.float32),
            pltpu.VMEM((n, drafts, cols), bf16),
            pltpu.VMEM((n, drafts, cols), bf16),
            dma((5,)),
            dma, dma,
            dma((pieces,)), dma((pieces,)),
            dma((pieces,)), dma((pieces,)),
            dma((depth,)), dma((depth,)),
            dma((depth,)), dma((depth,)),
            dma((depth,)), dma((depth,)),
            dma((n,)), dma((n,)),
        ],
        compiler_params=pltpu.CompilerParams(
            collective_id=0, has_side_effects=True, vmem_limit_bytes=56 * 1024 * 1024
        ),
    )(queries[0], cache[0].T, draft_latent[0], lengths, parents, value_up, out_proj)


def quad_of(mesh):
    line = mesh.devices.reshape(mesh.shape["grp"], mesh.shape["ctx"])[0]
    depth = len({d.coords[2] for d in line})
    return len(line) // depth


def solution(mesh):
    in_specs = (
        P("grp", None, "ctx", None),
        P("grp", "ctx", None),
        P("grp", None, None),
        P("grp"),
        P("grp", None),
        P("ctx", None, None),
        P("ctx", None),
    )
    out_specs = P("grp", "ctx")
    return jax.shard_map(
        functools.partial(on_device, quad_of(mesh), mesh.shape["ctx"]),
        mesh=mesh, in_specs=in_specs, out_specs=out_specs, check_vma=False,
    )
```

```python
import functools
import math

import jax
import jax.numpy as jnp
from jax import lax
from jax.experimental import pallas as pl
from jax.experimental.pallas import tpu as pltpu
from jax.sharding import PartitionSpec as P

yarn_factor = 1.0 + 0.1 * math.log(32.0)
score_scale = yarn_factor * yarn_factor / math.sqrt(192.0)
neg_fill = -1e30
MESH = pl.DeviceIdType.MESH
pieces = 4


def dot_nt(a, b):
    return lax.dot_general(a, b, (((1,), (1,)), ((), ())), preferred_element_type=jnp.float32)


def dot_nn(a, b):
    return lax.dot_general(a, b, (((1,), (0,)), ((), ())), preferred_element_type=jnp.float32)


def kernel(
    n, quad, heads, drafts, latent, width, vdim,
    q_hbm, cache_hbm, draft_hbm, lengths_ref, parents_ref, up_hbm, proj_hbm,
    out_ref,
    qraw, qsplit, qbuf, kv, draft, up, proj, acc, state_out, state_in, stat_out, stat_in,
    share, kept, pair_out, pair_in, share_out, share_in,
    from_up, from_down, load_sem, own_send, own_recv, near_send, near_recv, relay_send, relay_recv,
    q_send, q_recv, st_send, st_recv, stat_send, stat_recv,
    pair_send, pair_recv, share_send, share_recv,
):
    me = lax.axis_index("ctx")
    depth = n // quad
    rows = drafts * heads
    block = cache_hbm.shape[1]
    piece = width // pieces
    z = lax.div(me, quad)
    q = lax.rem(me, quad)
    core = lax.rem(q, 2)
    other = q + 1 - 2 * core
    partner = z * quad + other
    two_chips = quad > 2
    near_q = lax.rem(q + 2, quad)
    near = z * quad + near_q
    near_other_q = near_q + 1 - 2 * core

    def load(src, dst, i):
        copy = pltpu.make_async_copy(src, dst, load_sem.at[i])
        copy.start()
        return copy

    get_kv = load(cache_hbm, kv.at[0], 0)
    get_q = load(q_hbm, qraw, 1)
    get_draft = load(draft_hbm, draft, 2)
    get_up = load(up_hbm, up, 3)
    get_proj = load(proj_hbm, proj, 4)

    barrier = pltpu.get_barrier_semaphore()

    def signal(sem, device):
        pl.semaphore_signal(sem, inc=1, device_id={"ctx": device}, device_id_type=MESH)

    last = depth - 1
    signal(barrier, partner)
    if two_chips:
        signal(barrier, near)

    @pl.when(z < last)
    def _():
        signal(barrier, me + quad)

    @pl.when(z > 0)
    def _():
        signal(barrier, me - quad)

    get_q.wait()
    for i in range(drafts):
        line = qraw[i].astype(jnp.float32)
        for c in range(0, width, 128):
            lanes = min(128, width - c)
            qsplit[c // 128, pl.ds(i * heads, heads), pl.ds(0, lanes)] = line[:, c : c + lanes]
    for h in range(heads):
        for c in range(0, width, 128):
            lanes = min(128, width - c)
            turned = qsplit[c // 128, pl.ds(h, drafts, stride=heads), :]
            qbuf[0, pl.ds(h * drafts, drafts), pl.ds(c, lanes)] = turned[:, :lanes].astype(
                jnp.bfloat16
            )

    ends = lax.div(z + last, depth) + lax.div(last - z + last, depth)
    pl.semaphore_wait(barrier, ends + (2 if two_chips else 1))

    def remote(src, dst, send, recv, device):
        copy = pltpu.make_async_remote_copy(
            src_ref=src, dst_ref=dst, send_sem=send, recv_sem=recv,
            device_id={"ctx": device}, device_id_type=MESH,
        )
        copy.start()
        return copy

    sent = []
    near_copies = []
    if two_chips:
        for c in range(pieces):
            part = pl.ds(c * piece, piece)
            near_copies.append(remote(
                cache_hbm.at[part], kv.at[2, part], near_send.at[c], near_recv.at[c], near
            ))
    own = remote(cache_hbm, kv.at[1], own_send, own_recv, partner)

    for r in range(1, last):
        @pl.when((z >= 1) & (z + r <= last))
        def _():
            signal(from_up.at[r], me - quad)

        @pl.when((z < last) & (z >= r))
        def _():
            signal(from_down.at[r], me + quad)

        @pl.when(z + 1 + r <= last)
        def _():
            pl.semaphore_wait(from_up.at[r], 1)

        @pl.when(z >= 1 + r)
        def _():
            pl.semaphore_wait(from_down.at[r], 1)

    q_copies = []
    for o in range(1, depth):
        dest = lax.rem(z + o, depth) * quad + q
        q_copies.append(remote(qbuf.at[0], qbuf.at[o], q_send.at[o], q_recv.at[o], dest))

    row_id = lax.broadcasted_iota(jnp.int32, (drafts, drafts), 0)
    col_id = lax.broadcasted_iota(jnp.int32, (drafts, drafts), 1)
    eye = jnp.where(row_id == col_id, 1.0, 0.0)
    reach = jnp.where(row_id == jnp.broadcast_to(parents_ref[...], (drafts, drafts)), 1.0, eye)
    for _ in range(max(1, math.ceil(math.log2(drafts)))):
        low = reach.astype(jnp.bfloat16)
        reach = jnp.minimum(dot_nn(low, low), 1.0)
    reach = lax.dot_general(
        reach.astype(jnp.bfloat16), eye.astype(jnp.bfloat16), (((0,), (0,)), ((), ())),
        preferred_element_type=jnp.float32,
    )
    tree = jnp.concatenate([reach] * heads, axis=0) > 0.5
    get_draft.wait()
    keys = draft[...]
    d_score = jnp.where(tree, dot_nt(qbuf[0], keys) * score_scale, neg_fill)
    d_top = jnp.max(d_score, axis=1, keepdims=True)
    d_weight = jnp.where(tree, jnp.exp(d_score - d_top), 0.0).astype(jnp.bfloat16)
    d_total = jnp.sum(d_weight.astype(jnp.float32), axis=1, keepdims=True)
    d_numer = dot_nn(d_weight, keys[:, :latent])

    relays = []

    def relay(c):
        if two_chips:
            part = pl.ds(c * piece, piece)
            near_copies[c].wait_recv()
            relays.append(remote(
                kv.at[2, part], kv.at[3, part], relay_send.at[c], relay_recv.at[c], partner
            ))

    limit = lengths_ref[...]
    joined = rows % 8 == 0 and depth <= 8
    groups = [(0, depth)] if joined else [(o, 1) for o in range(depth)]
    tops = {}
    totals = {}

    def attend(slot, owner_q):
        first = (z * quad + owner_q) * block
        live = (first + lax.broadcasted_iota(jnp.int32, (1, block), 1)) < limit
        for base, count in groups:
            span = count * rows
            query = qbuf[pl.ds(base, count)].reshape(span, width)
            scores = jnp.where(live, dot_nn(query, kv[slot]) * score_scale, neg_fill)
            top = jnp.max(scores, axis=1, keepdims=True)
            place = pl.ds(base * rows, span)
            if base in tops:
                best = jnp.maximum(tops[base], top)
                decay = jnp.exp(tops[base] - best)
            else:
                best = top
            weights = jnp.where(live, jnp.exp(scores - best), 0.0).astype(jnp.bfloat16)
            total = jnp.sum(weights.astype(jnp.float32), axis=1, keepdims=True)
            numer = dot_nt(weights, kv[slot, pl.ds(0, latent), :])
            if base in tops:
                totals[base] = totals[base] * decay + total
                acc[place] = acc[place] * decay + numer
            else:
                totals[base] = total
                acc[place] = numer
            tops[base] = best

    for c in range(0, pieces - 2):
        relay(c)
    for copy in q_copies:
        copy.wait_recv()
    get_kv.wait()
    attend(0, q)
    own.wait_recv()
    relay(pieces - 2)
    attend(1, other)
    relay(pieces - 1)
    if two_chips:
        attend(2, near_q)
        for copy in relays:
            copy.wait_recv()
        attend(3, near_other_q)

    lane = lax.broadcasted_iota(jnp.int32, (rows, 128), 1)
    fill = jnp.zeros((128 - rows, 128), jnp.float32)
    state_copies = []
    stat_copies = []

    def stats_of(o):
        base, count = next(g for g in groups if g[0] <= o < g[0] + g[1])
        at = (o - base) * rows
        return tops[base][at : at + rows], totals[base][at : at + rows]

    for o in range(1, depth):
        top, total = stats_of(o)
        state_out[o] = acc[pl.ds(o * rows, rows)].astype(jnp.bfloat16)
        column = jnp.where(lane == 0, top, jnp.where(lane == 1, total, 0.0))
        stat_out[o] = jnp.concatenate([column, fill], axis=0).T[:8]
        back = depth - o
        dest = lax.rem(z + back, depth) * quad + q
        state_copies.append(remote(
            state_out.at[o], state_in.at[back], st_send.at[o], st_recv.at[back], dest
        ))
        stat_copies.append(remote(
            stat_out.at[o], stat_in.at[back], stat_send.at[o], stat_recv.at[back], dest
        ))

    def arrived(buf, send, recv, slot):
        return pltpu.make_async_remote_copy(
            src_ref=buf.at[slot], dst_ref=buf.at[slot], send_sem=send.at[slot],
            recv_sem=recv.at[slot], device_id={"ctx": partner}, device_id_type=MESH,
        )

    top0, total0 = stats_of(0)
    for s in range(1, depth):
        arrived(stat_in, stat_send, stat_recv, s).wait_recv()
    shown = jnp.concatenate(
        [stat_in[s] for s in range(1, depth)]
        + [jnp.zeros((-(depth - 1) * 8 % 128, 128), jnp.float32)], axis=0
    ).T
    their_top = [None] + [shown[:rows, 8 * s : 8 * s + 1] for s in range(depth - 1)]
    their_total = [None] + [shown[:rows, 8 * s + 1 : 8 * s + 2] for s in range(depth - 1)]
    best = jnp.maximum(top0, d_top)
    for s in range(1, depth):
        best = jnp.maximum(best, their_top[s])
    f0, fd = jnp.exp(top0 - best), jnp.exp(d_top - best)
    total = total0 * f0 + d_total * fd
    numer = acc[pl.ds(0, rows)] * f0 + d_numer * fd
    for s in range(1, depth):
        factor = jnp.exp(their_top[s] - best)
        total = total + their_total[s] * factor
        arrived(state_in, st_send, st_recv, s).wait_recv()
        numer = numer + state_in[s].astype(jnp.float32) * factor
    latent_out = (numer / total).astype(jnp.bfloat16).astype(jnp.float32)

    get_up.wait()
    values = [
        dot_nn(
            latent_out[h * drafts : (h + 1) * drafts].astype(jnp.bfloat16), up[h]
        ).astype(jnp.bfloat16)
        for h in range(heads)
    ]
    flat = jnp.concatenate(values, axis=1) if heads > 1 else values[0]

    cols = share_in.shape[2]
    per = 128 // math.gcd(cols, 128)
    per = per if per % 2 == 0 else 2 * per
    half = per // 2
    n_groups = n // per
    mine, seat = lax.div(me, per), lax.rem(me, per)
    chip = lax.div(seat, 2)
    order = list(range(1, n_groups)) + [0]
    share_copies = []
    pair_copies = {}
    lag = 3

    def project(j):
        target = lax.rem(mine + j, n_groups)
        start = pl.multiple_of(target * (per * cols), 128)
        product = dot_nn(flat, proj[:, pl.ds(start, per * cols)])
        for t in range(per):
            shifted = product if t == 0 else pltpu.roll(product, per * cols - t * cols, 1)
            share[j * per + t] = shifted[:, :cols]
            pair_out[j * per + t] = shifted[:, :cols].astype(jnp.bfloat16)
        for u in range(half):
            slot = j * half + u
            pair_copies[slot] = remote(
                pair_out.at[j * per + 2 * u + 1 - core], pair_in.at[slot],
                pair_send.at[slot], pair_recv.at[slot], partner,
            )

    def pass_on(j):
        target = lax.rem(mine + j, n_groups)
        for u in range(half):
            slot = j * half + u
            pair_copies[slot].wait_recv()
            both = share[j * per + 2 * u + core] + pair_in[slot].astype(jnp.float32)
            if j > 0:
                share_out[slot] = both.astype(jnp.bfloat16)
                place = j * half + chip
                share_copies.append(remote(
                    share_out.at[slot], share_in.at[place],
                    share_send.at[slot], share_recv.at[place], target * per + 2 * u + core,
                ))
            else:
                kept[u] = both
                share_out[slot] = both.astype(jnp.bfloat16)
        if j == 0:
            for d in range(1, half):
                u = lax.rem(chip + d, half)
                share_copies.append(remote(
                    share_out.at[u], share_in.at[d],
                    share_send.at[d], share_recv.at[d], mine * per + 2 * u + core,
                ))

    get_proj.wait()
    for i, j in enumerate(order):
        project(j)
        if i >= lag:
            pass_on(order[i - lag])
    for j in order[max(0, n_groups - lag):]:
        pass_on(j)
    result = kept[chip]
    for s in range(1, n // 2):
        arrived(share_in, share_send, share_recv, s).wait_recv()
        result = result + share_in[s].astype(jnp.float32)
    out_ref[...] = result.astype(jnp.bfloat16)

    for copy in pair_copies.values():
        copy.wait_send()
    own.wait_send()
    for copy in near_copies + relays + q_copies + state_copies + stat_copies + share_copies:
        copy.wait_send()


def on_device(quad, n, queries, cache, draft_latent, lengths, parents, value_up, out_proj):
    _, drafts, heads, width = queries.shape
    block = cache.shape[1]
    latent, vdim = value_up.shape[1:]
    depth = n // quad
    rows = drafts * heads
    model = out_proj.shape[1]
    cols = model // n
    anywhere = pl.BlockSpec(memory_space=pl.ANY)
    in_vmem = pl.BlockSpec(memory_space=pltpu.VMEM)
    dma = pltpu.SemaphoreType.DMA
    bf16 = jnp.bfloat16
    return pl.pallas_call(
        functools.partial(kernel, n, quad, heads, drafts, latent, width, vdim),
        out_shape=jax.ShapeDtypeStruct((drafts, cols), bf16),
        in_specs=[anywhere, anywhere, anywhere, in_vmem, in_vmem, anywhere, anywhere],
        out_specs=in_vmem,
        scratch_shapes=[
            pltpu.VMEM((drafts, heads, width), bf16),
            pltpu.VMEM((pl.cdiv(width, 128), rows, 128), jnp.float32),
            pltpu.VMEM((depth, rows, width), bf16),
            pltpu.VMEM((quad, width, block), bf16),
            pltpu.VMEM((drafts, width), bf16),
            pltpu.VMEM((heads, latent, vdim), bf16),
            pltpu.VMEM((heads * vdim, model), bf16),
            pltpu.VMEM((depth * rows, latent), jnp.float32),
            pltpu.VMEM((depth, rows, latent), bf16),
            pltpu.VMEM((depth, rows, latent), bf16),
            pltpu.VMEM((depth, 8, 128), jnp.float32),
            pltpu.VMEM((depth, 8, 128), jnp.float32),
            pltpu.VMEM((n, drafts, cols), jnp.float32),
            pltpu.VMEM((n // 2, drafts, cols), jnp.float32),
            pltpu.VMEM((n, drafts, cols), bf16),
            pltpu.VMEM((n // 2, drafts, cols), bf16),
            pltpu.VMEM((n // 2, drafts, cols), bf16),
            pltpu.VMEM((n // 2, drafts, cols), bf16),
            pltpu.SemaphoreType.REGULAR((depth,)),
            pltpu.SemaphoreType.REGULAR((depth,)),
            dma((5,)),
            dma, dma,
            dma((pieces,)), dma((pieces,)),
            dma((pieces,)), dma((pieces,)),
            dma((depth,)), dma((depth,)),
            dma((depth,)), dma((depth,)),
            dma((depth,)), dma((depth,)),
            dma((n // 2,)), dma((n // 2,)),
            dma((n // 2,)), dma((n // 2,)),
        ],
        compiler_params=pltpu.CompilerParams(
            collective_id=0, has_side_effects=True, vmem_limit_bytes=56 * 1024 * 1024
        ),
    )(queries[0], cache[0].T, draft_latent[0], lengths.reshape(1, 1), parents, value_up, out_proj)


def quad_of(mesh):
    line = mesh.devices.reshape(mesh.shape["grp"], mesh.shape["ctx"])[0]
    depth = len({d.coords[2] for d in line})
    return len(line) // depth


def solution(mesh):
    in_specs = (
        P("grp", None, "ctx", None),
        P("grp", "ctx", None),
        P("grp", None, None),
        P("grp"),
        P("grp", None),
        P("ctx", None, None),
        P("ctx", None),
    )
    out_specs = P("grp", "ctx")
    return jax.shard_map(
        functools.partial(on_device, quad_of(mesh), mesh.shape["ctx"]),
        mesh=mesh, in_specs=in_specs, out_specs=out_specs, check_vma=False,
    )
```
